256 devices in a mesh: dp: 64 (over z_hi, x, y, core), slab: 4 (over z_lo).
Axes of the slice: x: 4, y: 4, z: 8 (z_hi: 2, z_lo: 4; z = z_hi * 4 + z_lo), core: 2. Of those that a mesh axis runs over, the one named last changes fastest.
Arguments:
- images: bfloat16 [64, 256, 32, 128], P('dp', 'slab'), may hold values from -6 to 6
- cotangent: bfloat16 [64, 128, 64, 256], P('dp', None, 'slab'), may hold values from -6 to 6
- kernel: bfloat16 [3, 3, 256, 128], replicated, may hold values from -0.125 to 0.125
Outputs:
- grad_images: bfloat16 [64, 256, 32, 128], P('dp', 'slab')
- grad_kernel: float32 [3, 3, 256, 128], replicated
The draws below stay inside these ranges and needn't reach their ends.
All inputs are finite; a program needn't handle non-finite values.
Results may differ from the reference program's by a relative error of at most 0.0034.
Values may be sent and summed in bfloat16 or wider, within the bound.
No kernel may reach another device: no remote copies, remote signals or barrier semaphores. Data moves between devices by JAX's collectives and lax.ppermute only.
A program may use at most 64 MiB of HBM per device.

```python
import jax
import jax.numpy as jnp
from jax import lax

CIN = 256
COUT = 128
H_LO = 32
W_LO = 128
IMAGES = 64
H_UP = 64
W_UP = 256


def block_scale(rng, extent, cuts, low, largest):
    factor_of = 1.0
    for position, shards_of in cuts:
        heights = jax.random.uniform(jax.random.fold_in(jax.random.fold_in(rng, 6), position), (shards_of,), jnp.float32, low / len(cuts), largest / len(cuts))
        factor_of = factor_of * jnp.repeat(jnp.exp(heights), extent[position] // shards_of).reshape((-1,) + (1,) * (len(extent) - 1 - position))
    return factor_of


def centred(stream_key, shape, width, bound, split=(), dtype=jnp.bfloat16):
    factor_of = block_scale(stream_key, shape, split, -0.22, 0.18) if split else 1.0
    result = jax.random.normal(stream_key, shape, jnp.float32) * width * factor_of
    return jnp.minimum(jnp.maximum(result, -bound), bound).astype(dtype)


def setup_inputs(seed: int = 0) -> dict:
    keys = jax.random.split(jax.random.key(seed), 4)
    return {
        "images": centred(keys[0], (IMAGES, CIN, H_LO, W_LO), 1.0, 6.0, ((0, 64), (1, 4))),
        "cotangent": centred(keys[1], (IMAGES, COUT, H_UP, W_UP), 1.0, 6.0, ((0, 64), (2, 4))),
        "kernel": centred(keys[2], (3, 3, CIN, COUT), (9 * CIN) ** -0.5, 0.125),
    }


def upsample(field):
    return jnp.repeat(jnp.repeat(field, 2, axis=2), 2, axis=3)


def downsum(field):
    count, chans, rows, cols = field.shape
    return field.reshape(count, chans, rows // 2, 2, cols // 2, 2).sum(axis=(3, 5))


def kernel_terms(padded_up, grad_rows):
    return lax.conv_general_dilated(padded_up, grad_rows, (1, 1), ((0, 0), (1, 1)), dimension_numbers=("CNHW", "IOHW", "HWNC"), preferred_element_type=jnp.float32)


def input_terms(padded_grad, kernel):
    flipped = kernel[::-1, ::-1]
    return lax.conv_general_dilated(padded_grad, flipped, (1, 1), ((0, 0), (1, 1)), dimension_numbers=("NCHW", "HWOI", "NCHW"), preferred_element_type=jnp.float32)


def reference(images, cotangent, kernel):
    batch_img = images.reshape(IMAGES, 1, CIN, H_LO, W_LO)
    batch_grad = cotangent.reshape(IMAGES, 1, COUT, H_UP, W_UP)

    def step(total, pair):
        block_img, block_grad = pair
        upsampled = upsample(block_img)
        padded_up = jnp.pad(upsampled, ((0, 0), (0, 0), (1, 1), (0, 0)))
        padded_grad = jnp.pad(block_grad, ((0, 0), (0, 0), (1, 1), (0, 0)))
        total = total + kernel_terms(padded_up, block_grad)
        grad_low = downsum(input_terms(padded_grad, kernel)).astype(jnp.bfloat16)
        return total, grad_low

    start = jnp.zeros((3, 3, CIN, COUT), jnp.float32)
    grad_kernel, grad_low = lax.scan(step, start, (batch_img, batch_grad))
    return grad_low.reshape(IMAGES, CIN, H_LO, W_LO), grad_kernel
```

```python
import functools

import jax
import jax.numpy as jnp
from jax import lax
from jax.experimental import pallas as pl
from jax.experimental.pallas import tpu as pltpu
from jax.sharding import Mesh
from jax.sharding import PartitionSpec as P

BF = jnp.bfloat16
F32 = jnp.float32
NT = (((1,), (1,)), ((), ()))


def picker():
    col = lax.broadcasted_iota(jnp.int32, (256, 384), 0)
    n = lax.broadcasted_iota(jnp.int32, (256, 384), 1)
    start = 2 * (n & 127) + 1 - (n >> 7)
    return jnp.where((col == start) | (col == start + 1), 1.0, 0.0).astype(BF)


def stacked(wide):
    return jnp.concatenate([wide[:, 128 * b : 128 * b + 128] for b in range(3)], axis=0)


def pool_kernel(cot_ref, d_ref, y_ref):
    pick = picker()
    for i in range(8):
        part = jnp.dot(cot_ref[pl.ds(256 * i, 256), :], pick, preferred_element_type=F32)
        for b in range(3):
            y_ref[b, pl.ds(256 * i, 256), :] = part[:, 128 * b : 128 * b + 128]
    for b in range(3):
        above = None
        for p in range(8):
            even = y_ref[b, pl.ds(2 * p, 128, stride=16), :]
            odd = y_ref[b, pl.ds(2 * p + 1, 128, stride=16), :]
            upper = even if above is None else above + even
            d_ref[pl.ds(128 * (6 + b), 128), pl.ds(128 * p, 128)] = upper.astype(BF)
            d_ref[pl.ds(128 * (3 + b), 128), pl.ds(128 * p, 128)] = (even + odd).astype(BF)
            if p > 0:
                d_ref[pl.ds(128 * b, 128), pl.ds(128 * (p - 1), 128)] = upper.astype(BF)
            above = odd
        d_ref[pl.ds(128 * b, 128), pl.ds(896, 128)] = above.astype(BF)


def products(pixels, d_ref, edge_ref, out_ref):
    for k in range(0, 9, 3):
        part = lax.dot_general(pixels, d_ref[pl.ds(128 * k, 384), :], NT, preferred_element_type=F32)
        if k != 3:
            p = 7 if k == 0 else 0
            edge = edge_ref[pl.ds(64 * k, 384), :]
            part += lax.dot_general(
                pixels[:, 128 * p : 128 * p + 128], edge, NT, preferred_element_type=F32
            )
        for u in range(3):
            out_ref[pl.ds(128 * (k + u), 128), :] = part[:, 128 * u : 128 * u + 128]


def rows_of(m_ref, half):
    return m_ref[pl.ds(pl.multiple_of(half * 128, 128), 128), :]


def send_kernel(core_ref, img_ref, d_ref, top_ref, bot_ref, send_ref, m_ref, edge_ref, f_ref):
    pick = picker()
    edge_ref[pl.ds(0, 384), :] = stacked(jnp.dot(bot_ref[...], pick, preferred_element_type=F32)).astype(BF)
    edge_ref[pl.ds(384, 384), :] = stacked(jnp.dot(top_ref[...], pick, preferred_element_type=F32)).astype(BF)
    f_ref[...] = img_ref[...].astype(F32)
    for p in range(8):
        m_ref[:, pl.ds(128 * p, 128)] = f_ref[pl.ds(p, 256, stride=8), :].astype(BF)
    products(rows_of(m_ref, 1 - core_ref[0]), d_ref, edge_ref, send_ref)


def keep_kernel(core_ref, m_ref, d_ref, edge_ref, keep_ref):
    products(rows_of(m_ref, core_ref[0]), d_ref, edge_ref, keep_ref)


def join_kernel(keep_ref, came_ref, half_ref):
    half_ref[...] = (keep_ref[...] + came_ref[...]).astype(BF)


def fold_kernel(count, copies, x_ref, out_ref):
    rows = x_ref.shape[0] // count
    total = x_ref[pl.ds(0, rows), :].astype(F32)
    for k in range(1, count):
        total += x_ref[pl.ds(rows * k, rows), :].astype(F32)
    total = total.astype(out_ref.dtype)
    for k in range(copies):
        out_ref[pl.ds(rows * k, rows), :] = total


def image_kernel(slab_ref, ker_ref, d_ref, top_ref, bot_ref, *refs):
    f_ref = refs[4]
    pick = picker()
    edges = {
        0: (6, stacked(jnp.dot(top_ref[...], pick, preferred_element_type=F32)).astype(BF)),
        7: (0, stacked(jnp.dot(bot_ref[...], pick, preferred_element_type=F32)).astype(BF)),
    }
    weights = jnp.concatenate([ker_ref[k] for k in range(9)], axis=1)
    for h in range(4):
        part = jnp.dot(weights, d_ref[:, pl.ds(256 * h, 256)], preferred_element_type=F32)
        for p in (2 * h, 2 * h + 1):
            cells = part[:, 128 * (p % 2) : 128 * (p % 2) + 128]
            if p in edges:
                k, edge = edges[p]
                cells += jnp.dot(weights[:, 128 * k : 128 * k + 384], edge, preferred_element_type=F32)
            f_ref[pl.ds(p, 256, stride=8), :] = cells
    for k in range(4):
        place = pl.multiple_of((slab_ref[0] ^ k) * 512, 512)
        refs[k][...] = f_ref[pl.ds(place, 512), :].astype(BF)


def call(kernel, outs, scratch, flops, scalars, *args):
    spec = pl.BlockSpec(memory_space=pltpu.VMEM)
    ins = [pl.BlockSpec(memory_space=pltpu.SMEM)] * scalars + [spec] * (len(args) - scalars)
    sizes = sum(a.size * a.dtype.itemsize for a in args) + sum(o.size * o.dtype.itemsize for o in outs)
    return pl.pallas_call(
        kernel,
        out_shape=tuple(outs),
        in_specs=ins,
        out_specs=tuple([spec] * len(outs)),
        scratch_shapes=scratch,
        compiler_params=pltpu.CompilerParams(vmem_limit_bytes=24 << 20),
        cost_estimate=pl.CostEstimate(flops=flops, bytes_accessed=sizes, transcendentals=0),
    )(*args)


SWAP = [(0, 1), (1, 0)]
DOWN = [(0, 1), (1, 2), (2, 3)]
UP = [(1, 0), (2, 1), (3, 2)]


def fold(x, copies, dtype):
    count, rows, lanes = x.shape
    (out,) = call(
        functools.partial(fold_kernel, count, copies),
        [jax.ShapeDtypeStruct((copies * rows, lanes), dtype)], [], x.size, 0, x.reshape(count * rows, lanes),
    )
    return out.reshape(copies, rows, lanes)


def exchange(x, axes):
    return lax.all_to_all(x, axes, split_axis=0, concat_axis=0, tiled=True)


def body(images, cotangent, kernel):
    S = jax.ShapeDtypeStruct
    cot = cotangent[0]
    top = lax.ppermute(cot[:, 15, :], "s", DOWN)
    bot = lax.ppermute(cot[:, 0, :], "s", UP)
    blocks = images.reshape(64, 4, 8, 128).transpose(1, 0, 2, 3)
    img = exchange(blocks, "s").reshape(2048, 128)
    (d,) = call(
        pool_kernel, [S((1152, 1024), BF)],
        [pltpu.VMEM((3, 2048, 128), F32)], 450000000, 0, cot.reshape(2048, 256),
    )
    core, slab = lax.axis_index("c"), lax.axis_index("s")
    place = core.reshape(1).astype(jnp.int32)
    send, pixels, edges = call(
        send_kernel, [S((1152, 128), F32), S((256, 1024), BF), S((768, 128), BF)],
        [pltpu.VMEM((2048, 128), F32)], 300000000, 1, place, img, d, top, bot,
    )
    (keep,) = call(keep_kernel, [S((1152, 128), F32)], [], 300000000, 1, place, pixels, d, edges)
    low = call(
        image_kernel, [S((512, 128), BF)] * 4, [pltpu.VMEM((2048, 128), F32)],
        600000000, 1, slab.reshape(1).astype(jnp.int32), kernel.reshape(9, 256, 128), d, top, bot,
    )
    across = lax.axis_size("x") * lax.axis_size("y")
    along = lax.axis_size("zh") * lax.axis_size("s")
    rows = 1152 // across
    came = lax.ppermute(send, "c", SWAP)
    (half,) = call(join_kernel, [S((1152, 128), BF)], [], 150000, 0, keep, came)
    half = exchange(half.reshape(across, rows, 128), ("x", "y"))
    part = fold(half, along, F32)
    part = exchange(part, ("zh", "s"))
    part = fold(part, across, BF)
    mine = exchange(part, ("x", "y"))
    mine = mine.reshape(9, 128, 128)
    other = lax.ppermute(mine, "c", SWAP)
    first = core == 0
    total = jnp.concatenate([jnp.where(first, mine, other), jnp.where(first, other, mine)], axis=1)
    came = [low[0]] + [
        lax.ppermute(low[k], "s", [(i, i ^ k) for i in range(4)]) for k in (1, 2, 3)
    ]
    came = [x.reshape(64, 8, 128) for x in came]
    tiles = []
    for i in range(4):
        k = slab ^ i
        tiles.append(
            jnp.where(k == 0, came[0], jnp.where(k == 1, came[1], jnp.where(k == 2, came[2], came[3])))
        )
    grad_low = jnp.stack(tiles, axis=1).reshape(1, 64, 32, 128)
    return grad_low, total.astype(F32).reshape(3, 3, 256, 128)


def solution(mesh):
    fine = Mesh(mesh.devices.reshape(2, 4, 4, 2, 4), ("zh", "x", "y", "c", "s"))
    dp = ("zh", "x", "y", "c")
    placed = (P(dp, "s", None, None), P(dp, None, "s", None), P())
    return jax.shard_map(
        body,
        mesh=fine,
        in_specs=placed,
        out_specs=(P(dp, "s", None, None), P()),
        check_vma=False,
    )
```

```python
import functools

import jax
import jax.numpy as jnp
from jax import lax
from jax.experimental import pallas as pl
from jax.experimental.pallas import tpu as pltpu
from jax.sharding import Mesh
from jax.sharding import PartitionSpec as P

BF = jnp.bfloat16
F32 = jnp.float32
NT = (((1,), (1,)), ((), ()))


def picker():
    col = lax.broadcasted_iota(jnp.int32, (256, 384), 0)
    n = lax.broadcasted_iota(jnp.int32, (256, 384), 1)
    start = 2 * (n & 127) + 1 - (n >> 7)
    return jnp.where((col == start) | (col == start + 1), 1.0, 0.0).astype(BF)


def stacked(wide):
    return jnp.concatenate([wide[:, 128 * b : 128 * b + 128] for b in range(3)], axis=0)


def pool_kernel(cot_ref, d_ref, y_ref):
    pick = picker()
    for i in range(8):
        part = jnp.dot(cot_ref[pl.ds(256 * i, 256), :], pick, preferred_element_type=F32)
        for b in range(3):
            y_ref[b, pl.ds(256 * i, 256), :] = part[:, 128 * b : 128 * b + 128]
    for b in range(3):
        above = None
        for p in range(8):
            even = y_ref[b, pl.ds(2 * p, 128, stride=16), :]
            odd = y_ref[b, pl.ds(2 * p + 1, 128, stride=16), :]
            upper = even if above is None else above + even
            d_ref[pl.ds(128 * (6 + b), 128), pl.ds(128 * p, 128)] = upper.astype(BF)
            d_ref[pl.ds(128 * (3 + b), 128), pl.ds(128 * p, 128)] = (even + odd).astype(BF)
            if p > 0:
                d_ref[pl.ds(128 * b, 128), pl.ds(128 * (p - 1), 128)] = upper.astype(BF)
            above = odd
        d_ref[pl.ds(128 * b, 128), pl.ds(896, 128)] = above.astype(BF)


def products(pixels, d_ref, edge_ref, out_ref):
    for k in range(0, 9, 3):
        part = lax.dot_general(pixels, d_ref[pl.ds(128 * k, 384), :], NT, preferred_element_type=F32)
        if k != 3:
            p = 7 if k == 0 else 0
            edge = edge_ref[pl.ds(64 * k, 384), :]
            part += lax.dot_general(
                pixels[:, 128 * p : 128 * p + 128], edge, NT, preferred_element_type=F32
            )
        for u in range(3):
            out_ref[pl.ds(128 * (k + u), 128), :] = part[:, 128 * u : 128 * u + 128]


def rows_of(m_ref, half):
    return m_ref[pl.ds(pl.multiple_of(half * 128, 128), 128), :]


def part_kernel(slab_ref, images_ref, *refs):
    sems = refs[4]
    copies = []
    for k in (3, 2, 1, 0):
        place = pl.multiple_of((slab_ref[0] ^ k) * 8, 8)
        copy = pltpu.make_async_copy(images_ref.at[:, pl.ds(place, 8), :], refs[k], sems.at[k])
        copy.start()
        copies.append(copy)
    for copy in copies:
        copy.wait()


def send_kernel(core_ref, slab_ref, *refs):
    d_ref, top_ref, bot_ref, send_ref, m_ref, edge_ref, f_ref = refs[4:]
    pick = picker()
    edge_ref[pl.ds(0, 384), :] = stacked(jnp.dot(bot_ref[...], pick, preferred_element_type=F32)).astype(BF)
    edge_ref[pl.ds(384, 384), :] = stacked(jnp.dot(top_ref[...], pick, preferred_element_type=F32)).astype(BF)
    for k in range(4):
        place = pl.multiple_of((slab_ref[0] ^ k) * 512, 512)
        f_ref[pl.ds(place, 512), :] = refs[k][...].astype(F32)
    for p in range(8):
        m_ref[:, pl.ds(128 * p, 128)] = f_ref[pl.ds(p, 256, stride=8), :].astype(BF)
    products(rows_of(m_ref, 1 - core_ref[0]), d_ref, edge_ref, send_ref)


def keep_kernel(core_ref, m_ref, d_ref, edge_ref, keep_ref):
    products(rows_of(m_ref, core_ref[0]), d_ref, edge_ref, keep_ref)


def join_kernel(keep_ref, came_ref, half_ref):
    half_ref[...] = (keep_ref[...] + came_ref[...]).astype(BF)


def fold_kernel(count, copies, x_ref, out_ref):
    rows = x_ref.shape[0] // count
    total = x_ref[pl.ds(0, rows), :].astype(F32)
    for k in range(1, count):
        total += x_ref[pl.ds(rows * k, rows), :].astype(F32)
    total = total.astype(out_ref.dtype)
    for k in range(copies):
        out_ref[pl.ds(rows * k, rows), :] = total


def image_kernel(slab_ref, ker_ref, d_ref, top_ref, bot_ref, *refs):
    f_ref = refs[4]
    pick = picker()
    edges = {
        0: (6, stacked(jnp.dot(top_ref[...], pick, preferred_element_type=F32)).astype(BF)),
        7: (0, stacked(jnp.dot(bot_ref[...], pick, preferred_element_type=F32)).astype(BF)),
    }
    weights = jnp.concatenate([ker_ref[k] for k in range(9)], axis=1)
    for h in range(4):
        part = jnp.dot(weights, d_ref[:, pl.ds(256 * h, 256)], preferred_element_type=F32)
        for p in (2 * h, 2 * h + 1):
            cells = part[:, 128 * (p % 2) : 128 * (p % 2) + 128]
            if p in edges:
                k, edge = edges[p]
                cells += jnp.dot(weights[:, 128 * k : 128 * k + 384], edge, preferred_element_type=F32)
            f_ref[pl.ds(p, 256, stride=8), :] = cells
    for k in range(4):
        place = pl.multiple_of((slab_ref[0] ^ k) * 512, 512)
        refs[k][...] = f_ref[pl.ds(place, 512), :].astype(BF)


def call(kernel, outs, scratch, flops, scalars, *args):
    spec = pl.BlockSpec(memory_space=pltpu.VMEM)
    ins = [pl.BlockSpec(memory_space=pltpu.SMEM)] * scalars + [spec] * (len(args) - scalars)
    sizes = sum(a.size * a.dtype.itemsize for a in args) + sum(o.size * o.dtype.itemsize for o in outs)
    return pl.pallas_call(
        kernel,
        out_shape=tuple(outs),
        in_specs=ins,
        out_specs=tuple([spec] * len(outs)),
        scratch_shapes=scratch,
        compiler_params=pltpu.CompilerParams(vmem_limit_bytes=24 << 20),
        cost_estimate=pl.CostEstimate(flops=flops, bytes_accessed=sizes, transcendentals=0),
    )(*args)


SWAP = [(0, 1), (1, 0)]
DOWN = [(0, 1), (1, 2), (2, 3)]
UP = [(1, 0), (2, 1), (3, 2)]


def fold(x, copies, dtype):
    count, rows, lanes = x.shape
    (out,) = call(
        functools.partial(fold_kernel, count, copies),
        [jax.ShapeDtypeStruct((copies * rows, lanes), dtype)], [], x.size, 0, x.reshape(count * rows, lanes),
    )
    return out.reshape(copies, rows, lanes)


def swapped(x, k):
    return lax.ppermute(x, "s", [(i, i ^ k) for i in range(4)])


def exchange(x, axes):
    return lax.all_to_all(x, axes, split_axis=0, concat_axis=0, tiled=True)


def body(images, cotangent, kernel):
    S = jax.ShapeDtypeStruct
    cot = cotangent[0]
    core = lax.axis_index("c").reshape(1).astype(jnp.int32)
    slab = lax.axis_index("s").reshape(1).astype(jnp.int32)
    blocks = pl.pallas_call(
        part_kernel,
        out_shape=(S((64, 8, 128), BF),) * 4,
        in_specs=[pl.BlockSpec(memory_space=pltpu.SMEM), pl.BlockSpec(memory_space=pltpu.HBM)],
        out_specs=(pl.BlockSpec(memory_space=pltpu.VMEM),) * 4,
        scratch_shapes=[pltpu.SemaphoreType.DMA((4,))],
        compiler_params=pltpu.CompilerParams(vmem_limit_bytes=8 << 20),
        cost_estimate=pl.CostEstimate(flops=0, bytes_accessed=1048576, transcendentals=0),
        name="parted",
    )(slab, images[0])
    img = {k: swapped(blocks[k], k) for k in (3, 2, 1)}
    img = [x.reshape(512, 128) for x in (blocks[0], img[1], img[2], img[3])]
    top = lax.ppermute(cot[:, 15, :], "s", DOWN)
    bot = lax.ppermute(cot[:, 0, :], "s", UP)
    (d,) = call(
        pool_kernel, [S((1152, 1024), BF)],
        [pltpu.VMEM((3, 2048, 128), F32)], 450000000, 0, cot.reshape(2048, 256),
    )
    send, pixels, edges = call(
        send_kernel, [S((1152, 128), F32), S((256, 1024), BF), S((768, 128), BF)],
        [pltpu.VMEM((2048, 128), F32)], 300000000, 2, core, slab, *img, d, top, bot,
    )
    (keep,) = call(keep_kernel, [S((1152, 128), F32)], [], 300000000, 1, core, pixels, d, edges)
    low = call(
        image_kernel, [S((512, 128), BF)] * 4, [pltpu.VMEM((2048, 128), F32)],
        600000000, 1, slab, kernel.reshape(9, 256, 128), d, top, bot,
    )
    across = lax.axis_size("x") * lax.axis_size("y")
    along = lax.axis_size("zh") * lax.axis_size("s")
    rows = 1152 // across
    came = lax.ppermute(send, "c", SWAP)
    (half,) = call(join_kernel, [S((1152, 128), BF)], [], 150000, 0, keep, came)
    half = exchange(half.reshape(across, rows, 128), ("x", "y"))
    part = fold(half, along, F32)
    part = exchange(part, ("zh", "s"))
    part = fold(part, across, BF)
    mine = exchange(part, ("x", "y"))
    mine = mine.reshape(9, 128, 128)
    other = lax.ppermute(mine, "c", SWAP)
    first = core[0] == 0
    total = jnp.concatenate([jnp.where(first, mine, other), jnp.where(first, other, mine)], axis=1)
    came = [low[0]]
    for k in (1, 2, 3):
        came.append(swapped(low[k], k))
    came = [x.reshape(64, 8, 128) for x in came]
    tiles = []
    for i in range(4):
        k = slab[0] ^ i
        tiles.append(
            jnp.where(k == 0, came[0], jnp.where(k == 1, came[1], jnp.where(k == 2, came[2], came[3])))
        )
    grad_low = jnp.stack(tiles, axis=1).reshape(1, 64, 32, 128)
    return grad_low, total.astype(F32).reshape(3, 3, 256, 128)


def solution(mesh):
    fine = Mesh(mesh.devices.reshape(2, 4, 4, 2, 4), ("zh", "x", "y", "c", "s"))
    dp = ("zh", "x", "y", "c")
    placed = (P(dp, "s", None, None), P(dp, None, "s", None), P())
    return jax.shard_map(
        body,
        mesh=fine,
        in_specs=placed,
        out_specs=(P(dp, "s", None, None), P()),
        check_vma=False,
    )
```

```python
import functools

import jax
import jax.numpy as jnp
from jax import lax
from jax.experimental import pallas as pl
from jax.experimental.pallas import tpu as pltpu
from jax.sharding import Mesh
from jax.sharding import PartitionSpec as P

BF = jnp.bfloat16
F32 = jnp.float32
NT = (((1,), (1,)), ((), ()))


def picker():
    col = lax.broadcasted_iota(jnp.int32, (256, 384), 0)
    n = lax.broadcasted_iota(jnp.int32, (256, 384), 1)
    start = 2 * (n & 127) + 1 - (n >> 7)
    return jnp.where((col == start) | (col == start + 1), 1.0, 0.0).astype(BF)


def stacked(wide):
    return jnp.concatenate([wide[:, 128 * b : 128 * b + 128] for b in range(3)], axis=0)


def ends_kernel(cot_ref, last_ref, first_ref):
    line = lax.broadcasted_iota(jnp.int32, (32, 256), 0)
    col = lax.broadcasted_iota(jnp.int32, (32, 256), 1)
    want = jnp.where(line < 16, 16 * line + 15, 16 * (line - 16))
    pick = jnp.where(col == want, 1.0, 0.0).astype(BF)
    for i in range(8):
        part = jnp.dot(pick, cot_ref[pl.ds(256 * i, 256), :], preferred_element_type=F32).astype(BF)
        last_ref[pl.ds(16 * i, 16), :] = part[:16]
        first_ref[pl.ds(16 * i, 16), :] = part[16:]


def pool_kernel(cot_ref, d_ref, e_ref, y_ref):
    pick = picker()
    for i in range(8):
        part = jnp.dot(cot_ref[pl.ds(256 * i, 256), :], pick, preferred_element_type=F32)
        for b in range(3):
            y_ref[b, pl.ds(256 * i, 256), :] = part[:, 128 * b : 128 * b + 128]
    for b in range(3):
        above = None
        for p in range(8):
            even = y_ref[b, pl.ds(2 * p, 128, stride=16), :]
            odd = y_ref[b, pl.ds(2 * p + 1, 128, stride=16), :]
            upper = even if above is None else above + even
            cells = [(6 + b, p, upper), (3 + b, p, even + odd)]
            if p > 0:
                cells.append((b, p - 1, upper))
            if p == 7:
                cells.append((b, 7, odd))
            above = odd
            for k, q, value in cells:
                high = value.astype(BF)
                d_ref[pl.ds(128 * k, 128), pl.ds(128 * q, 128)] = high
                e_ref[pl.ds(128 * k, 128), pl.ds(128 * q, 128)] = (value - high.astype(F32)).astype(BF)


def products(pixels, d_ref, e_ref, edge_ref, out_ref):
    for k in range(0, 9, 3):
        part = lax.dot_general(pixels, d_ref[pl.ds(128 * k, 384), :], NT, preferred_element_type=F32)
        part += lax.dot_general(pixels, e_ref[pl.ds(128 * k, 384), :], NT, preferred_element_type=F32)
        if k != 3:
            p = 7 if k == 0 else 0
            edge = edge_ref[pl.ds(64 * k, 384), :]
            part += lax.dot_general(
                pixels[:, 128 * p : 128 * p + 128], edge, NT, preferred_element_type=F32
            )
        for u in range(3):
            out_ref[pl.ds(128 * (k + u), 128), :] = part[:, 128 * u : 128 * u + 128]


def rows_of(m_ref, half):
    return m_ref[pl.ds(pl.multiple_of(half * 128, 128), 128), :]


def part_kernel(slab_ref, images_ref, *refs):
    sems = refs[4]
    copies = []
    for k in (3, 2, 1, 0):
        place = pl.multiple_of((slab_ref[0] ^ k) * 8, 8)
        copy = pltpu.make_async_copy(images_ref.at[:, pl.ds(place, 8), :], refs[k], sems.at[k])
        copy.start()
        copies.append(copy)
    for copy in copies:
        copy.wait()


def send_kernel(core_ref, slab_ref, *refs):
    d_ref, e_ref, top_ref, bot_ref, send_ref, m_ref, edge_ref, f_ref = refs[4:]
    pick = picker()
    edge_ref[pl.ds(0, 384), :] = stacked(jnp.dot(bot_ref[...], pick, preferred_element_type=F32)).astype(BF)
    edge_ref[pl.ds(384, 384), :] = stacked(jnp.dot(top_ref[...], pick, preferred_element_type=F32)).astype(BF)
    for k in range(4):
        place = pl.multiple_of((slab_ref[0] ^ k) * 512, 512)
        f_ref[pl.ds(place, 512), :] = refs[k][...].astype(F32)
    for p in range(8):
        m_ref[:, pl.ds(128 * p, 128)] = f_ref[pl.ds(p, 256, stride=8), :].astype(BF)
    products(rows_of(m_ref, 1 - core_ref[0]), d_ref, e_ref, edge_ref, send_ref)


def keep_kernel(core_ref, m_ref, d_ref, e_ref, edge_ref, keep_ref):
    products(rows_of(m_ref, core_ref[0]), d_ref, e_ref, edge_ref, keep_ref)


def join_kernel(keep_ref, came_ref, half_ref):
    half_ref[...] = (keep_ref[...] + came_ref[...]).astype(BF)


def fold_kernel(count, copies, x_ref, out_ref):
    rows = x_ref.shape[0] // count
    total = x_ref[pl.ds(0, rows), :].astype(F32)
    for k in range(1, count):
        total += x_ref[pl.ds(rows * k, rows), :].astype(F32)
    total = total.astype(out_ref.dtype)
    for k in range(copies):
        out_ref[pl.ds(rows * k, rows), :] = total


def image_kernel(slab_ref, ker_ref, d_ref, top_ref, bot_ref, *refs):
    f_ref = refs[4]
    pick = picker()
    edges = {
        0: (6, stacked(jnp.dot(top_ref[...], pick, preferred_element_type=F32)).astype(BF)),
        7: (0, stacked(jnp.dot(bot_ref[...], pick, preferred_element_type=F32)).astype(BF)),
    }
    weights = jnp.concatenate([ker_ref[k] for k in range(9)], axis=1)
    for h in range(4):
        part = jnp.dot(weights, d_ref[:, pl.ds(256 * h, 256)], preferred_element_type=F32)
        for p in (2 * h, 2 * h + 1):
            cells = part[:, 128 * (p % 2) : 128 * (p % 2) + 128]
            if p in edges:
                k, edge = edges[p]
                cells += jnp.dot(weights[:, 128 * k : 128 * k + 384], edge, preferred_element_type=F32)
            f_ref[pl.ds(p, 256, stride=8), :] = cells
    for k in range(4):
        place = pl.multiple_of((slab_ref[0] ^ k) * 512, 512)
        refs[k][...] = f_ref[pl.ds(place, 512), :].astype(BF)


def call(kernel, outs, scratch, flops, scalars, *args):
    spec = pl.BlockSpec(memory_space=pltpu.VMEM)
    ins = [pl.BlockSpec(memory_space=pltpu.SMEM)] * scalars + [spec] * (len(args) - scalars)
    sizes = sum(a.size * a.dtype.itemsize for a in args) + sum(o.size * o.dtype.itemsize for o in outs)
    return pl.pallas_call(
        kernel,
        out_shape=tuple(outs),
        in_specs=ins,
        out_specs=tuple([spec] * len(outs)),
        scratch_shapes=scratch,
        compiler_params=pltpu.CompilerParams(vmem_limit_bytes=24 << 20),
        cost_estimate=pl.CostEstimate(flops=flops, bytes_accessed=sizes, transcendentals=0),
    )(*args)


SWAP = [(0, 1), (1, 0)]
DOWN = [(0, 1), (1, 2), (2, 3)]
UP = [(1, 0), (2, 1), (3, 2)]


def fold(x, copies, dtype):
    count, rows, lanes = x.shape
    (out,) = call(
        functools.partial(fold_kernel, count, copies),
        [jax.ShapeDtypeStruct((copies * rows, lanes), dtype)], [], x.size, 0, x.reshape(count * rows, lanes),
    )
    return out.reshape(copies, rows, lanes)


def swapped(x, k):
    return lax.ppermute(x, "s", [(i, i ^ k) for i in range(4)])


def exchange(x, axes):
    return lax.all_to_all(x, axes, split_axis=0, concat_axis=0, tiled=True)


def body(images, cotangent, kernel):
    S = jax.ShapeDtypeStruct
    cot = cotangent[0]
    core = lax.axis_index("c").reshape(1).astype(jnp.int32)
    slab = lax.axis_index("s").reshape(1).astype(jnp.int32)
    blocks = pl.pallas_call(
        part_kernel,
        out_shape=(S((64, 8, 128), BF),) * 4,
        in_specs=[pl.BlockSpec(memory_space=pltpu.SMEM), pl.BlockSpec(memory_space=pltpu.HBM)],
        out_specs=(pl.BlockSpec(memory_space=pltpu.VMEM),) * 4,
        scratch_shapes=[pltpu.SemaphoreType.DMA((4,))],
        compiler_params=pltpu.CompilerParams(vmem_limit_bytes=8 << 20),
        cost_estimate=pl.CostEstimate(flops=0, bytes_accessed=1048576, transcendentals=0),
        name="parted",
    )(slab, pltpu.with_memory_space_constraint(images[0], pltpu.HBM))
    img = {k: swapped(blocks[k], k) for k in (3, 2, 1)}
    img = [x.reshape(512, 128) for x in (blocks[0], img[1], img[2], img[3])]
    rows_in = cot.reshape(2048, 256)
    last, first = call(ends_kernel, [S((128, 256), BF)] * 2, [], 34000000, 0, rows_in)
    top = lax.ppermute(last, "s", DOWN)
    bot = lax.ppermute(first, "s", UP)
    d, e = call(
        pool_kernel, [S((1152, 1024), BF)] * 2,
        [pltpu.VMEM((3, 2048, 128), F32)], 450000000, 0, cot.reshape(2048, 256),
    )
    send, pixels, edges = call(
        send_kernel, [S((1152, 128), F32), S((256, 1024), BF), S((768, 128), BF)],
        [pltpu.VMEM((2048, 128), F32)], 300000000, 2, core, slab, *img, d, e, top, bot,
    )
    (keep,) = call(keep_kernel, [S((1152, 128), F32)], [], 300000000, 1, core, pixels, d, e, edges)
    low = call(
        image_kernel, [S((512, 128), BF)] * 4, [pltpu.VMEM((2048, 128), F32)],
        600000000, 1, slab, kernel.reshape(9, 256, 128), d, top, bot,
    )
    across = lax.axis_size("x") * lax.axis_size("y")
    along = lax.axis_size("zh") * lax.axis_size("s")
    rows = 1152 // across
    came = lax.ppermute(send, "c", SWAP)
    (half,) = call(join_kernel, [S((1152, 128), BF)], [], 150000, 0, keep, came)
    half = exchange(half.reshape(across, rows, 128), ("x", "y"))
    part = fold(half, along, BF)
    part = exchange(part, ("zh", "s"))
    part = fold(part, across, BF)
    mine = exchange(part, ("x", "y"))
    mine = mine.reshape(9, 128, 128)
    other = lax.ppermute(mine, "c", SWAP)
    first = core[0] == 0
    total = jnp.concatenate([jnp.where(first, mine, other), jnp.where(first, other, mine)], axis=1)
    came = [low[0]]
    for k in (1, 2, 3):
        came.append(swapped(low[k], k))
    came = [x.reshape(64, 8, 128) for x in came]
    tiles = []
    for i in range(4):
        k = slab[0] ^ i
        tiles.append(
            jnp.where(k == 0, came[0], jnp.where(k == 1, came[1], jnp.where(k == 2, came[2], came[3])))
        )
    grad_low = jnp.stack(tiles, axis=1).reshape(1, 64, 32, 128)
    return grad_low, total.astype(F32).reshape(3, 3, 256, 128)


def solution(mesh):
    fine = Mesh(mesh.devices.reshape(2, 4, 4, 2, 4), ("zh", "x", "y", "c", "s"))
    dp = ("zh", "x", "y", "c")
    placed = (P(dp, "s", None, None), P(dp, None, "s", None), P())
    return jax.shard_map(
        body,
        mesh=fine,
        in_specs=placed,
        out_specs=(P(dp, "s", None, None), P()),
        check_vma=False,
    )
```

```python
import functools

import jax
import jax.numpy as jnp
from jax import lax
from jax.experimental import pallas as pl
from jax.experimental.pallas import tpu as pltpu
from jax.sharding import Mesh
from jax.sharding import PartitionSpec as P

BF = jnp.bfloat16
F32 = jnp.float32
NT = (((1,), (1,)), ((), ()))


def picker():
    col = lax.broadcasted_iota(jnp.int32, (256, 384), 0)
    n = lax.broadcasted_iota(jnp.int32, (256, 384), 1)
    start = 2 * (n & 127) + 1 - (n >> 7)
    return jnp.where((col == start) | (col == start + 1), 1.0, 0.0).astype(BF)


def stacked(wide):
    return jnp.concatenate([wide[:, 128 * b : 128 * b + 128] for b in range(3)], axis=0)


def ends_kernel(cot_ref, last_ref, first_ref):
    line = lax.broadcasted_iota(jnp.int32, (32, 256), 0)
    col = lax.broadcasted_iota(jnp.int32, (32, 256), 1)
    want = jnp.where(line < 16, 16 * line + 15, 16 * (line - 16))
    pick = jnp.where(col == want, 1.0, 0.0).astype(BF)
    for i in range(8):
        part = jnp.dot(pick, cot_ref[pl.ds(256 * i, 256), :], preferred_element_type=F32).astype(BF)
        last_ref[pl.ds(16 * i, 16), :] = part[:16]
        first_ref[pl.ds(16 * i, 16), :] = part[16:]


def pool_kernel(cot_ref, d_ref, e_ref, y_ref):
    pick = picker()
    for i in range(8):
        part = jnp.dot(cot_ref[pl.ds(256 * i, 256), :], pick, preferred_element_type=F32)
        for b in range(3):
            y_ref[b, pl.ds(256 * i, 256), :] = part[:, 128 * b : 128 * b + 128]
    for b in range(3):
        above = None
        for p in range(8):
            even = y_ref[b, pl.ds(2 * p, 128, stride=16), :]
            odd = y_ref[b, pl.ds(2 * p + 1, 128, stride=16), :]
            upper = even if above is None else above + even
            cells = [(6 + b, p, upper), (3 + b, p, even + odd)]
            if p > 0:
                cells.append((b, p - 1, upper))
            if p == 7:
                cells.append((b, 7, odd))
            above = odd
            for k, q, value in cells:
                high = value.astype(BF)
                d_ref[pl.ds(128 * k, 128), pl.ds(128 * q, 128)] = high
                e_ref[pl.ds(128 * k, 128), pl.ds(128 * q, 128)] = (value - high.astype(F32)).astype(BF)


def products(pixels, d_ref, e_ref, edge_ref, out_ref):
    for k, count, edge, p in ((0, 2, 0, 7), (2, 1, 2, 7), (3, 2, None, 0), (5, 1, None, 0), (6, 2, 3, 0), (8, 1, 5, 0)):
        span = pl.ds(128 * k, 128 * count)
        part = lax.dot_general(pixels, d_ref[span, :], NT, preferred_element_type=F32)
        part += lax.dot_general(pixels, e_ref[span, :], NT, preferred_element_type=F32)
        if edge is not None:
            part += lax.dot_general(
                pixels[:, 128 * p : 128 * p + 128], edge_ref[pl.ds(128 * edge, 128 * count), :], NT,
                preferred_element_type=F32,
            )
        for u in range(count):
            out_ref[pl.ds(128 * (k + u), 128), :] = part[:, 128 * u : 128 * u + 128]


def rows_of(m_ref, half):
    return m_ref[pl.ds(pl.multiple_of(half * 128, 128), 128), :]


def part_kernel(slab_ref, images_ref, *refs):
    sems = refs[4]
    copies = []
    for k in (3, 2, 1, 0):
        place = pl.multiple_of((slab_ref[0] ^ k) * 8, 8)
        copy = pltpu.make_async_copy(images_ref.at[:, pl.ds(place, 8), :], refs[k], sems.at[k])
        copy.start()
        copies.append(copy)
    for copy in copies:
        copy.wait()


def send_kernel(core_ref, slab_ref, *refs):
    d_ref, e_ref, top_ref, bot_ref, send_ref, m_ref, edge_ref, f_ref = refs[4:]
    pick = picker()
    edge_ref[pl.ds(0, 384), :] = stacked(jnp.dot(bot_ref[...], pick, preferred_element_type=F32)).astype(BF)
    edge_ref[pl.ds(384, 384), :] = stacked(jnp.dot(top_ref[...], pick, preferred_element_type=F32)).astype(BF)
    for k in range(4):
        place = pl.multiple_of((slab_ref[0] ^ k) * 512, 512)
        f_ref[pl.ds(place, 512), :] = refs[k][...].astype(F32)
    for p in range(8):
        m_ref[:, pl.ds(128 * p, 128)] = f_ref[pl.ds(p, 256, stride=8), :].astype(BF)
    products(rows_of(m_ref, 1 - core_ref[0]), d_ref, e_ref, edge_ref, send_ref)


def keep_kernel(core_ref, m_ref, d_ref, e_ref, edge_ref, keep_ref):
    products(rows_of(m_ref, core_ref[0]), d_ref, e_ref, edge_ref, keep_ref)


def join_kernel(keep_ref, came_ref, half_ref):
    half_ref[...] = (keep_ref[...] + came_ref[...]).astype(BF)


def fold_kernel(count, copies, x_ref, out_ref):
    rows = x_ref.shape[0] // count
    total = x_ref[pl.ds(0, rows), :].astype(F32)
    for k in range(1, count):
        total += x_ref[pl.ds(rows * k, rows), :].astype(F32)
    total = total.astype(out_ref.dtype)
    for k in range(copies):
        out_ref[pl.ds(rows * k, rows), :] = total


def image_kernel(slab_ref, ker_ref, d_ref, top_ref, bot_ref, *refs):
    f_ref = refs[4]
    pick = picker()
    edges = {
        0: (6, stacked(jnp.dot(top_ref[...], pick, preferred_element_type=F32)).astype(BF)),
        7: (0, stacked(jnp.dot(bot_ref[...], pick, preferred_element_type=F32)).astype(BF)),
    }
    weights = jnp.concatenate([ker_ref[k] for k in range(9)], axis=1)
    for h in range(4):
        part = jnp.dot(weights, d_ref[:, pl.ds(256 * h, 256)], preferred_element_type=F32)
        for p in (2 * h, 2 * h + 1):
            cells = part[:, 128 * (p % 2) : 128 * (p % 2) + 128]
            if p in edges:
                k, edge = edges[p]
                cells += jnp.dot(weights[:, 128 * k : 128 * k + 384], edge, preferred_element_type=F32)
            f_ref[pl.ds(p, 256, stride=8), :] = cells
    for k in range(4):
        place = pl.multiple_of((slab_ref[0] ^ k) * 512, 512)
        refs[k][...] = f_ref[pl.ds(place, 512), :].astype(BF)


def call(kernel, outs, scratch, flops, scalars, *args):
    spec = pl.BlockSpec(memory_space=pltpu.VMEM)
    ins = [pl.BlockSpec(memory_space=pltpu.SMEM)] * scalars + [spec] * (len(args) - scalars)
    sizes = sum(a.size * a.dtype.itemsize for a in args) + sum(o.size * o.dtype.itemsize for o in outs)
    return pl.pallas_call(
        kernel,
        out_shape=tuple(outs),
        in_specs=ins,
        out_specs=tuple([spec] * len(outs)),
        scratch_shapes=scratch,
        compiler_params=pltpu.CompilerParams(vmem_limit_bytes=24 << 20),
        cost_estimate=pl.CostEstimate(flops=flops, bytes_accessed=sizes, transcendentals=0),
    )(*args)


SWAP = [(0, 1), (1, 0)]
DOWN = [(0, 1), (1, 2), (2, 3)]
UP = [(1, 0), (2, 1), (3, 2)]


def fold(x, copies, dtype):
    count, rows, lanes = x.shape
    (out,) = call(
        functools.partial(fold_kernel, count, copies),
        [jax.ShapeDtypeStruct((copies * rows, lanes), dtype)], [], x.size, 0, x.reshape(count * rows, lanes),
    )
    return out.reshape(copies, rows, lanes)


def swapped(x, k):
    return lax.ppermute(x, "s", [(i, i ^ k) for i in range(4)])


def exchange(x, axes):
    return lax.all_to_all(x, axes, split_axis=0, concat_axis=0, tiled=True)


def body(images, cotangent, kernel):
    S = jax.ShapeDtypeStruct
    cot = cotangent[0]
    core = lax.axis_index("c").reshape(1).astype(jnp.int32)
    slab = lax.axis_index("s").reshape(1).astype(jnp.int32)
    blocks = pl.pallas_call(
        part_kernel,
        out_shape=(S((64, 8, 128), BF),) * 4,
        in_specs=[pl.BlockSpec(memory_space=pltpu.SMEM), pl.BlockSpec(memory_space=pltpu.HBM)],
        out_specs=(pl.BlockSpec(memory_space=pltpu.VMEM),) * 4,
        scratch_shapes=[pltpu.SemaphoreType.DMA((4,))],
        compiler_params=pltpu.CompilerParams(vmem_limit_bytes=8 << 20),
        cost_estimate=pl.CostEstimate(flops=0, bytes_accessed=1048576, transcendentals=0),
        name="parted",
    )(slab, pltpu.with_memory_space_constraint(images[0], pltpu.HBM))
    img = {}
    for k in (3, 2, 1):
        img[k] = swapped(blocks[k], k)
    img = [x.reshape(512, 128) for x in (blocks[0], img[1], img[2], img[3])]
    rows_in = cot.reshape(2048, 256)
    last, first = call(ends_kernel, [S((128, 256), BF)] * 2, [], 34000000, 0, rows_in)
    top = lax.ppermute(last, "s", DOWN)
    bot = lax.ppermute(first, "s", UP)
    d, e = call(
        pool_kernel, [S((1152, 1024), BF)] * 2,
        [pltpu.VMEM((3, 2048, 128), F32)], 450000000, 0, cot.reshape(2048, 256),
    )
    send, pixels, edges = call(
        send_kernel, [S((1152, 128), F32), S((256, 1024), BF), S((768, 128), BF)],
        [pltpu.VMEM((2048, 128), F32)], 300000000, 2, core, slab, *img, d, e, top, bot,
    )
    (keep,) = call(keep_kernel, [S((1152, 128), F32)], [], 300000000, 1, core, pixels, d, e, edges)
    low = call(
        image_kernel, [S((512, 128), BF)] * 4, [pltpu.VMEM((2048, 128), F32)],
        600000000, 1, slab, kernel.reshape(9, 256, 128), d, top, bot,
    )
    across = lax.axis_size("x") * lax.axis_size("y")
    along = lax.axis_size("zh") * lax.axis_size("s")
    rows = 1152 // across
    came = lax.ppermute(send, "c", SWAP)
    (half,) = call(join_kernel, [S((1152, 128), BF)], [], 150000, 0, keep, came)
    half = exchange(half.reshape(across, rows, 128), ("x", "y"))
    part = fold(half, along, BF)
    part = exchange(part, ("zh", "s"))
    part = fold(part, across, BF)
    mine = exchange(part, ("x", "y"))
    mine = mine.reshape(9, 128, 128)
    other = lax.ppermute(mine, "c", SWAP)
    first = core[0] == 0
    total = jnp.concatenate([jnp.where(first, mine, other), jnp.where(first, other, mine)], axis=1)
    came = [low[0]]
    for k in (1, 2, 3):
        came.append(swapped(low[k], k))
    came = [x.reshape(64, 8, 128) for x in came]
    tiles = []
    for i in range(4):
        k = slab[0] ^ i
        tiles.append(
            jnp.where(k == 0, came[0], jnp.where(k == 1, came[1], jnp.where(k == 2, came[2], came[3])))
        )
    grad_low = jnp.stack(tiles, axis=1).reshape(1, 64, 32, 128)
    return grad_low, total.astype(F32).reshape(3, 3, 256, 128)


def solution(mesh):
    fine = Mesh(mesh.devices.reshape(2, 4, 4, 2, 4), ("zh", "x", "y", "c", "s"))
    dp = ("zh", "x", "y", "c")
    placed = (P(dp, "s", None, None), P(dp, None, "s", None), P())
    return jax.shard_map(
        body,
        mesh=fine,
        in_specs=placed,
        out_specs=(P(dp, "s", None, None), P()),
        check_vma=False,
    )
```
